512 devices in a mesh: gx: 16 (over x, z_lo), gy: 8 (over y, core), ga: 4 (over z_hi).
Axes of the slice: x: 4, y: 4, z: 16 (z_hi: 4, z_lo: 4; z = z_hi * 4 + z_lo), core: 2. Of those that a mesh axis runs over, the one named last changes fastest.
Arguments:
- mixture_fields_initial: float32 [16, 256, 256, 128], P(None, 'gx', ('gy', 'ga')), may hold values from 0 to 1
- flow_speed_vector: float32 [3, 256, 256, 128], P(None, 'gx', ('gy', 'ga')), may hold values from -2 to 2
- thermal_field: float32 [256, 256, 128], P('gx', ('gy', 'ga')), may hold values from 1 to 3
- mass_diffusivity: float32 [16], replicated, may hold values from 0.05 to 0.3
- arrhenius_constant: float32 [16], replicated, may hold values from 0.3 to 3
- arrhenius_energy_temp: float32 [16], replicated, may hold values from 0.5 to 4
- production_coefficients: float32 [16, 16], replicated, may hold values from -1.5 to 1.5
- tucker_factor_east: float32 [256, 64], P('gx'), may hold values from -1 to 1, as said below
- tucker_factor_north: float32 [256, 64], P(('gy', 'ga')), may hold values from -1 to 1, as said below
- tucker_factor_vertical: float32 [128, 32], replicated, may hold values from -1 to 1, as said below
- tucker_factor_component: float32 [16, 8], replicated, may hold values from -1 to 1, as said below
Outputs:
- mixture_fields_final: float32 [16, 256, 256, 128], P(None, 'gx', ('gy', 'ga'))
- residual: float32 [16, 256, 256, 128], P(None, 'gx', ('gy', 'ga'))
- tucker_core: float32 [8, 64, 64, 32], P(None, 'gx', ('gy', 'ga'))
The draws below stay inside these ranges and needn't reach their ends.
Inputs may be any that keep to these rules, and one draw needn't show every extreme that they name: tucker_factor_east has orthonormal columns. tucker_factor_north has orthonormal columns. tucker_factor_vertical has orthonormal columns. tucker_factor_component has orthonormal columns.
All inputs are finite; a program needn't handle non-finite values.
Results may differ from the reference program's by a relative error of at most 0.0001.
Values sent between devices are 32-bit elements; how exact they have to be, the bound alone decides.
A program may use at most 64 MiB of HBM per device.

```python
import math
import jax
import jax.numpy as jnp
from jax import lax

S = 16
RS = 8
RX = 64
RY = 64
RZ = 32
GRID_LENGTH_UP = 128
SUB = 2
GRID_LENGTH_EAST = 256
GRID_LENGTH_NORTH = 256


def orthonormal(key, rows, columns):
    matrix = jax.random.normal(key, (rows, columns), jnp.float32)
    return jnp.linalg.qr(matrix)[0]


def draw_tucker_factor_east(key, part):
    return orthonormal(jax.random.fold_in(key, 11), GRID_LENGTH_EAST, RX)


def draw_tucker_factor_north(key, part):
    return orthonormal(jax.random.fold_in(key, 12), GRID_LENGTH_NORTH, RY)


def draw_tucker_factor_vertical(key, part):
    return orthonormal(jax.random.fold_in(key, 13), GRID_LENGTH_UP, RZ)


def draw_tucker_factor_component(key, part):
    return orthonormal(jax.random.fold_in(key, 14), S, RS)


def level_of(rng, shape, shards, low, top_value):
    loudness, own = 1.0, jax.random.fold_in(rng, 6)
    for axis_at, shards_of in shards:
        heights = jnp.exp(jax.random.uniform(jax.random.fold_in(own, axis_at), (shards_of,), jnp.float32, low / len(shards), top_value / len(shards)))
        loudness = loudness * jnp.repeat(heights, shape[axis_at] // shards_of).reshape([-1 if axis == axis_at else 1 for axis in range(len(shape))])
    return loudness


def centred(key, extent, spread, most, shards=(), kind=jnp.bfloat16):
    gain = level_of(key, extent, shards, -0.22, 0.18) if shards else 1.0
    entries = jax.random.normal(key, extent, jnp.float32) * spread * gain
    return jnp.minimum(jnp.maximum(entries, -most), most).astype(kind)


def setup_inputs(seed: int = 0) -> dict:
    splits = jax.random.split(jax.random.key(seed), 12)
    mixture_fields_initial = jnp.clip(1.0 * jax.random.uniform(splits[0], (S, GRID_LENGTH_EAST, GRID_LENGTH_NORTH, GRID_LENGTH_UP), jnp.float32) ** level_of(splits[0], (S, GRID_LENGTH_EAST, GRID_LENGTH_NORTH, GRID_LENGTH_UP), ((1, 16), (2, 32)), -0.2, 0.2), 0.0, 1.0)
    flow_speed_vector = centred(splits[1], (3, GRID_LENGTH_EAST, GRID_LENGTH_NORTH, GRID_LENGTH_UP), 0.5, 2.0, ((1, 16), (2, 32)), jnp.float32)
    thermal_field = jnp.clip(1.0 + 2.0 * jax.random.uniform(splits[2], (GRID_LENGTH_EAST, GRID_LENGTH_NORTH, GRID_LENGTH_UP), jnp.float32) ** level_of(splits[2], (GRID_LENGTH_EAST, GRID_LENGTH_NORTH, GRID_LENGTH_UP), ((0, 16), (1, 32)), -0.2, 0.2), 1.0, 3.0)
    mass_diffusivity = jnp.clip(jnp.exp(jax.random.uniform(splits[3], (S,), jnp.float32, math.log(0.05), math.log(0.3))), 0.05, 0.3)
    arrhenius_constant = jnp.clip(jnp.exp(jax.random.uniform(splits[4], (S,), jnp.float32, math.log(0.3), math.log(3.0))), 0.3, 3.0)
    arrhenius_energy_temp = jnp.clip(jnp.exp(jax.random.uniform(splits[5], (S,), jnp.float32, math.log(0.5), math.log(4.0))), 0.5, 4.0)
    production_coefficients = centred(splits[6], (S, S), S ** -0.5, 1.5, (), jnp.float32)
    tucker_factor_east = draw_tucker_factor_east(jax.random.fold_in(splits[11], 71), 0)
    tucker_factor_north = draw_tucker_factor_north(jax.random.fold_in(splits[11], 71), 0)
    tucker_factor_vertical = draw_tucker_factor_vertical(jax.random.fold_in(splits[11], 71), 0)
    tucker_factor_component = draw_tucker_factor_component(jax.random.fold_in(splits[11], 71), 0)
    return dict(mixture_fields_initial=mixture_fields_initial, flow_speed_vector=flow_speed_vector, thermal_field=thermal_field, mass_diffusivity=mass_diffusivity, arrhenius_constant=arrhenius_constant, arrhenius_energy_temp=arrhenius_energy_temp, production_coefficients=production_coefficients, tucker_factor_east=tucker_factor_east, tucker_factor_north=tucker_factor_north, tucker_factor_vertical=tucker_factor_vertical, tucker_factor_component=tucker_factor_component)


time_step = 0.5

def advance_solution(tensor_elements, flow_speed_vector, thermal_field, mass_diffusivity, arrhenius_constant, arrhenius_energy_temp, production_coefficients):
    padded = jnp.pad(tensor_elements, ((0, 0), (1, 1), (1, 1), (0, 0)))
    x_plus = padded[:, 2:, 1:-1, :]
    x_minus = padded[:, :-2, 1:-1, :]
    y_plus = padded[:, 1:-1, 2:, :]
    y_minus = padded[:, 1:-1, :-2, :]
    zero_layer = jnp.zeros_like(tensor_elements[..., :1])
    z_plus = jnp.concatenate([tensor_elements[..., 1:], zero_layer], axis=3)
    z_minus = jnp.concatenate([zero_layer, tensor_elements[..., :-1]], axis=3)
    laplace = x_plus + x_minus + y_plus + y_minus + z_plus + z_minus - 6.0 * tensor_elements
    advect = 0.5 * (flow_speed_vector[0] * (x_plus - x_minus) + flow_speed_vector[1] * (y_plus - y_minus) + flow_speed_vector[2] * (z_plus - z_minus))
    swap_neighbour_halo = jnp.concatenate([tensor_elements[1:], tensor_elements[:1]], axis=0)
    reaction_source_terms = arrhenius_constant[:, None, None, None] * jnp.exp(-arrhenius_energy_temp[:, None, None, None] / thermal_field) * tensor_elements * swap_neighbour_halo
    produced = jnp.einsum('sk,kxyz->sxyz', production_coefficients, reaction_source_terms, precision=lax.Precision.HIGHEST)
    return tensor_elements + time_step * (mass_diffusivity[:, None, None, None] * laplace - advect + produced)

def reference(mixture_fields_initial, flow_speed_vector, thermal_field, mass_diffusivity, arrhenius_constant, arrhenius_energy_temp, production_coefficients, tucker_factor_east, tucker_factor_north, tucker_factor_vertical, tucker_factor_component):
    highest = lax.Precision.HIGHEST
    mixture_snapshot_record = mixture_fields_initial
    for substep in range(SUB):
        mixture_snapshot_record = advance_solution(mixture_snapshot_record, flow_speed_vector, thermal_field, mass_diffusivity, arrhenius_constant, arrhenius_energy_temp, production_coefficients)
    projected = jnp.einsum('sxyz,sa->axyz', mixture_snapshot_record, tucker_factor_component, precision=highest)
    projected = jnp.einsum('axyz,zd->axyd', projected, tucker_factor_vertical, precision=highest)
    projected = jnp.einsum('axyd,yc->axcd', projected, tucker_factor_north, precision=highest)
    tucker_core = jnp.einsum('axcd,xb->abcd', projected, tucker_factor_east, precision=highest)
    expanded = jnp.einsum('abcd,xb->axcd', tucker_core, tucker_factor_east, precision=highest)
    expanded = jnp.einsum('axcd,yc->axyd', expanded, tucker_factor_north, precision=highest)
    expanded = jnp.einsum('axyd,zd->axyz', expanded, tucker_factor_vertical, precision=highest)
    expanded = jnp.einsum('axyz,sa->sxyz', expanded, tucker_factor_component, precision=highest)
    residual = mixture_snapshot_record - expanded
    mixture_fields_final = mixture_snapshot_record
    for substep in range(SUB):
        mixture_fields_final = advance_solution(mixture_fields_final, flow_speed_vector, thermal_field, mass_diffusivity, arrhenius_constant, arrhenius_energy_temp, production_coefficients)
    return (mixture_fields_final, residual, tucker_core)
```

```python
import functools
import jax
import jax.numpy as jnp
from jax import lax
from jax.experimental import pallas as pl
from jax.experimental.pallas import tpu as pltpu
from jax.sharding import PartitionSpec as P

MESH = pl.DeviceIdType.MESH
HI = lax.Precision.HIGHEST
F32 = jnp.float32
SPECIES = 16
RANK_S = 8
NX = 16
NY = 8
NZ = 128
DX = 16
DY = 32
GA = 4
GY = 8
ZL = 4
CHUNKS = 4
CX = NX // CHUNKS
ORDER = (0, 3, 1, 2)


def dot(a, b):
    return lax.dot_general(a, b, (((1,), (0,)), ((), ())), precision=HI, preferred_element_type=F32)


def dot_tn(a, b):
    return lax.dot_general(a, b, (((0,), (0,)), ((), ())), precision=HI, preferred_element_type=F32)


def dot_nt(a, b):
    return lax.dot_general(a, b, (((1,), (1,)), ((), ())), precision=HI, preferred_element_type=F32)


def iota(shape, dim):
    return lax.broadcasted_iota(jnp.int32, shape, dim)


def kernel(
    v_hbm, flow_hbm, temp_hbm, diff_ref, pre_ref, energy_ref, prod_ref, comp_ref,
    east_ref, north_ref, vert_ref,
    final_hbm, resid_hbm, core_ref,
    V, F, T, K, PC, CC, HY, FY, S, VT, NF, EF,
    PB, G, QB, H, MB, Q8, UB, W, CS, CO, RES,
    load_sem, out_sem,
    sx, rx, sy, ry,
    sn1, rn1, sn2, rn2, se1, re1, se2, re2,
    sp, rp, sq, rq, sm, rm, su, ru, sc, rc,
):
    gx = lax.axis_index("gx")
    gy = lax.axis_index("gy")
    ga = lax.axis_index("ga")
    me = gy * GA + ga
    zl = lax.rem(gx, ZL)
    xh = gx // ZL

    def at_y(j):
        return {"gx": gx, "gy": j // GA, "ga": lax.rem(j, GA)}

    def at_x(m):
        return {"gx": m, "gy": gy, "ga": ga}

    barrier = pltpu.get_barrier_semaphore()

    def greet_y(k, c):
        pl.semaphore_signal(barrier, inc=1, device_id=at_y(lax.rem(me + k, DY)), device_id_type=MESH)
        return c

    def greet_x(k, c):
        pl.semaphore_signal(barrier, inc=1, device_id=at_x(lax.rem(gx + k, DX)), device_id_type=MESH)
        return c

    lax.fori_loop(1, DY, greet_y, 0)
    lax.fori_loop(1, DX, greet_x, 0)

    load_v = pltpu.make_async_copy(v_hbm, V.at[0, :, pl.ds(1, NX)], load_sem.at[0])
    load_f = pltpu.make_async_copy(flow_hbm, F, load_sem.at[1])
    load_t = pltpu.make_async_copy(temp_hbm, T, load_sem.at[2])
    load_v.start()
    load_f.start()
    load_t.start()

    zeros = jnp.zeros((SPECIES, NY, NZ), F32)
    zface = jnp.zeros((NX, SPECIES, NZ), F32)
    for n in range(4):
        @pl.when(gx == 0)
        def _():
            V[n, :, 0] = zeros

        @pl.when(gx == DX - 1)
        def _():
            V[n, :, NX + 1] = zeros

        @pl.when(me == 0)
        def _():
            HY[n, 0] = zface

        @pl.when(me == DY - 1)
        def _():
            HY[n, 1] = zface

    load_v.wait()

    def pack(x, c):
        for s in range(SPECIES):
            tile = V[0, s, x + 1]
            FY[0, 0, x, s:s + 1, :] = tile[0:1, :]
            FY[0, 1, x, s:s + 1, :] = tile[NY - 1:NY, :]
        return c

    lax.fori_loop(0, NX, pack, 0)
    pl.semaphore_wait(barrier, DY - 1 + DX - 1)

    def copy_x(n, up):
        return pltpu.make_async_remote_copy(
            src_ref=V.at[n, :, NX if up else 1],
            dst_ref=V.at[n, :, 0 if up else NX + 1],
            send_sem=sx.at[n, up],
            recv_sem=rx.at[n, up],
            device_id=at_x(gx + 1 if up else gx - 1),
            device_id_type=MESH,
        )

    def copy_y(n, up, c):
        part = pl.ds(c * CX, CX)
        return pltpu.make_async_remote_copy(
            src_ref=FY.at[n, up, part],
            dst_ref=HY.at[n, 1 - up, part],
            send_sem=sy.at[n, up, c],
            recv_sem=ry.at[n, up, c],
            device_id=at_y(me + 1 if up else me - 1),
            device_id_type=MESH,
        )

    def has(axis_up):
        axis, up = axis_up
        if axis == "x":
            return gx < DX - 1 if up else gx > 0
        return me < DY - 1 if up else me > 0

    def send_x(n, up):
        @pl.when(has(("x", up)))
        def _():
            copy_x(n, up).start()

    def send_y(n, c):
        for up in (0, 1):
            @pl.when(has(("y", up)))
            def _():
                copy_y(n, up, c).start()

    def recv_x(n, up):
        @pl.when(has(("x", 1 - up)))
        def _():
            copy_x(n, up).wait_recv()

    def recv_y(n, c):
        for up in (0, 1):
            @pl.when(has(("y", 1 - up)))
            def _():
                copy_y(n, up, c).wait_recv()

    send_x(0, 0)
    send_x(0, 1)
    for c in ORDER:
        send_y(0, c)

    old = iota((64, 128), 0)
    spread = (iota((64, 128), 1) == (old >> 2) * 8 + (old & 3)).astype(F32)
    NF[me] = dot(north_ref[...], spread)
    eye = (iota((64, 128), 1) == iota((64, 128), 0)).astype(F32)
    EF[gx] = dot(east_ref[...], eye)

    def n1(k):
        return pltpu.make_async_remote_copy(
            NF.at[me], NF.at[me], sn1, rn1,
            device_id=at_y(gy * GA + lax.rem(ga + k, GA)), device_id_type=MESH)

    def n2(k):
        part = pl.ds(gy * GA, GA)
        return pltpu.make_async_remote_copy(
            NF.at[part], NF.at[part], sn2, rn2,
            device_id=at_y(lax.rem(gy + k, GY) * GA + ga), device_id_type=MESH)

    def e1(k):
        return pltpu.make_async_remote_copy(
            EF.at[gx], EF.at[gx], se1, re1,
            device_id=at_x(xh * ZL + lax.rem(zl + k, ZL)), device_id_type=MESH)

    def e2(k):
        part = pl.ds(xh * ZL, ZL)
        return pltpu.make_async_remote_copy(
            EF.at[part], EF.at[part], se2, re2,
            device_id=at_x(lax.rem(xh + k, DX // ZL) * ZL + zl), device_id_type=MESH)

    for k in range(1, GA):
        n1(k).start()
    for k in range(1, ZL):
        e1(k).start()

    def taken(ref, send, recv):
        return pltpu.make_async_remote_copy(
            ref, ref, send, recv, device_id=at_y(lax.rem(me + 1, DY)), device_id_type=MESH)

    load_t.wait()
    load_f.wait()

    def rates(x, c):
        inverse = 1.0 / T[x]
        for k in range(SPECIES):
            K[k, x] = (0.5 * pre_ref[k]) * jnp.exp((-energy_ref[k]) * inverse)
        for d in range(3):
            F[d, x] = 0.25 * F[d, x]
        return c

    lax.fori_loop(0, NX, rates, 0)

    def splat(s, c):
        for k in range(SPECIES):
            PC[s * SPECIES + k] = jnp.full((8, 128), prod_ref[s, k], F32)
        for a in range(RANK_S):
            CC[s * RANK_S + a] = jnp.full((8, 128), comp_ref[s, a], F32)
        return c

    lax.fori_loop(0, SPECIES, splat, 0)

    spot = iota((32, 512), 1)
    pick = (iota((32, 512), 0) == (spot >> 7) * 8 + (spot & 7)).astype(F32)
    VT[...] = dot(vert_ref[...], pick)

    row = iota((NY, NZ), 0)
    lane = iota((NY, NZ), 1)

    def advance(n, x, last):
        vs = [V[n, s, x + 1] for s in range(SPECIES)]
        react = [K[k, x] * vs[k] * vs[(k + 1) % SPECIES] for k in range(SPECIES)]
        fx, fy, fz = F[0, x], F[1, x], F[2, x]
        for s in range(SPECIES):
            v = vs[s]
            xp, xm = V[n, s, x + 2], V[n, s, x]
            up = jnp.broadcast_to(HY[n, 1, x, s:s + 1, :], (NY, NZ))
            down = jnp.broadcast_to(HY[n, 0, x, s:s + 1, :], (NY, NZ))
            yp = jnp.where(row == NY - 1, up, pltpu.roll(v, NY - 1, 0))
            ym = jnp.where(row == 0, down, pltpu.roll(v, 1, 0))
            zp = jnp.where(lane == NZ - 1, 0.0, pltpu.roll(v, NZ - 1, 1))
            zm = jnp.where(lane == 0, 0.0, pltpu.roll(v, 1, 1))
            half = 0.5 * diff_ref[s]
            total = (1.0 - 6.0 * half) * v + half * ((xp + xm) + (yp + ym) + (zp + zm))
            total = total - (fx * (xp - xm) + fy * (yp - ym) + fz * (zp - zm))
            made = PC[s * SPECIES] * react[0]
            for k in range(1, SPECIES):
                made = made + PC[s * SPECIES + k] * react[k]
            total = total + made
            V[n + 1, s, x + 1] = total
            if not last:
                FY[n + 1, 0, x, s:s + 1, :] = total[0:1, :]
                FY[n + 1, 1, x, s:s + 1, :] = total[NY - 1:NY, :]

    def step(n, c):
        last = n == 3
        recv_y(n, c)
        if c == 0:
            recv_x(n, 1)
        if c == CHUNKS - 1:
            recv_x(n, 0)

        def body(i, carry):
            advance(n, c * CX + i, last)
            return carry

        lax.fori_loop(0, CX, body, 0)
        if not last:
            send_y(n + 1, c)
            if c == 0:
                send_x(n + 1, 0)
            if c == CHUNKS - 1:
                send_x(n + 1, 1)
        else:
            save(c).start()

    def save(c):
        return pltpu.make_async_copy(
            V.at[4, :, pl.ds(1 + c * CX, CX)],
            final_hbm.at[:, pl.ds(c * CX, CX)],
            out_sem.at[c])

    step(0, ORDER[0])
    taken(NF.at[pl.ds(0, GA - 1)], sn1, rn1).wait()
    for k in range(1, GY):
        n2(k).start()
    taken(EF.at[pl.ds(0, ZL - 1)], se1, re1).wait()
    for k in range(1, DX // ZL):
        e2(k).start()
    for c in ORDER[1:]:
        step(0, c)
    for c in ORDER:
        step(1, c)

    def squash(x, carry):
        vs = [V[2, s, x + 1] for s in range(SPECIES)]
        for a in range(RANK_S):
            total = CC[a] * vs[0]
            for s in range(1, SPECIES):
                total = total + CC[s * RANK_S + a] * vs[s]
            S[a, x] = total
        return carry

    lax.fori_loop(0, NX, squash, 0)
    wide = ((iota((NX, NY, 512), 2) & 127) >> 3) == iota((NX, NY, 512), 0)

    def project(a, carry):
        out = dot(S[a].reshape(NX * NY, NZ), VT[...]).reshape(NX, NY, 512)
        out = jnp.sum(jnp.where(wide, out, 0.0), axis=0)
        for d in range(4):
            PB[a * 4 + d] = out[:, d * 128:(d + 1) * 128]
        return carry

    lax.fori_loop(0, RANK_S, project, 0)

    def to_y(src, dst, send, recv):
        def go(k, carry):
            j = lax.rem(me + k, DY)
            pltpu.make_async_remote_copy(
                src.at[j], dst.at[me], send, recv, device_id=at_y(j), device_id_type=MESH).start()
            return carry
        lax.fori_loop(1, DY, go, 0)

    def to_x(src, dst, send, recv):
        def go(k, carry):
            m = lax.rem(gx + k, DX)
            pltpu.make_async_remote_copy(
                src.at[m], dst.at[gx], send, recv, device_id=at_x(m), device_id_type=MESH).start()
            return carry
        lax.fori_loop(1, DX, go, 0)

    def done_y(ref, send, recv):
        taken(ref.at[pl.ds(0, DY - 1)], send, recv).wait()

    def done_x(ref, send, recv):
        taken(ref.at[pl.ds(0, DX - 1)], send, recv).wait()

    to_y(PB, G, sp, rp)
    G[me] = PB[me]

    for c in ORDER:
        step(2, c)

    taken(NF.at[pl.ds(0, GA * (GY - 1))], sn2, rn2).wait()
    taken(EF.at[pl.ds(0, ZL * (DX // ZL - 1))], se2, re2).wait()
    done_y(G, sp, rp)
    north = NF[...].reshape(DY * NY, 128)
    QB[...] = dot_tn(north, G[...].reshape(DY * NY, 128)).reshape(DX, 8, 128)
    to_x(QB, H, sq, rq)
    H[gx] = QB[gx]

    step(3, ORDER[0])

    done_x(H, sq, rq)
    own_x = (iota((DX, NX, 128), 2) >> 3) == iota((DX, NX, 128), 1)
    blocks = []
    for c in range(4):
        spread_h = jnp.broadcast_to(H[:, c:c + 1, :], (DX, NX, 128))
        blocks.append(jnp.where(own_x, spread_h, 0.0).reshape(DX * NX, 128))
    east = EF[...].reshape(DX * NX, 128)
    core = dot_tn(east, jnp.concatenate(blocks, axis=1))
    piece = jnp.zeros((128, 128), F32)
    slot = iota((128, 128), 1) >> 3
    b_low = iota((128, 128), 0) & 3
    parts = []
    for c in range(4):
        part = core[:, c * 128:(c + 1) * 128]
        for shift in (64, 32, 16, 8):
            part = part + pltpu.roll(part, shift, 1)
        parts.append(part)
        piece = piece + jnp.where(slot == c * 4 + b_low, part, 0.0)
    out = dot(east, jnp.concatenate(parts, axis=1))
    for c in range(4):
        block = out[:, c * 128:(c + 1) * 128].reshape(DX, NX, 128)
        MB[:, c, :] = jnp.sum(jnp.where(own_x, block, 0.0), axis=1)
    MB[:, 4, :] = jnp.sum(piece[:64].reshape(DX, 4, 128), axis=1)
    for c in range(5, 8):
        MB[:, c, :] = jnp.zeros((DX, 128), F32)
    to_x(MB, Q8, sm, rm)
    Q8[gx] = MB[gx]

    step(3, ORDER[1])

    done_x(Q8, sm, rm)
    UB[...] = dot(NF[...].reshape(DY * NY, 128), Q8[...].reshape(DX * 8, 128)).reshape(DY, NY, 128)
    to_y(UB, W, su, ru)
    W[me] = UB[me]
    for m in range(DX):
        CS[m] = Q8[m, 4:5, :]
    own = CO.at[lax.rem(me, 4) * 8 + me // 4]

    def core_go(k, carry):
        j = lax.rem(me + k, DY)
        pltpu.make_async_remote_copy(
            CS.at[j // 2], own, sc, rc, device_id=at_y(j), device_id_type=MESH).start()
        return carry

    lax.fori_loop(1, DY, core_go, 0)
    CO[lax.rem(me, 4) * 8 + me // 4] = CS[me // 2]

    step(3, ORDER[2])
    step(3, ORDER[3])

    done_y(W, su, ru)
    tall = (iota((NX, NY, 128), 2) >> 3) == iota((NX, NY, 128), 0)

    def rebuild(a, carry):
        left = []
        for d in range(4):
            copies = jnp.broadcast_to(W[a * 4 + d][None], (NX, NY, 128))
            left.append(jnp.where(tall, copies, 0.0).reshape(NX * NY, 128))
        S[a] = dot_nt(jnp.concatenate(left, axis=1), VT[...]).reshape(NX, NY, NZ)
        return carry

    lax.fori_loop(0, RANK_S, rebuild, 0)

    def spill(c):
        return pltpu.make_async_copy(
            RES.at[:, pl.ds(c * CX, CX)], resid_hbm.at[:, pl.ds(c * CX, CX)], out_sem.at[CHUNKS + c])

    def subtract(x, carry):
        rs = [S[a, x] for a in range(RANK_S)]
        for s in range(SPECIES):
            total = V[2, s, x + 1]
            for a in range(RANK_S):
                total = total - CC[s * RANK_S + a] * rs[a]
            RES[s, x] = total
        return carry

    for c in range(CHUNKS):
        lax.fori_loop(c * CX, (c + 1) * CX, subtract, 0)
        spill(c).start()

    taken(CO.at[pl.ds(0, DY - 1)], sc, rc).wait()
    odd = lax.rem(me, 2)
    result = jnp.zeros((8, 256), F32)
    src_lane = iota((128, 256), 0)
    dst_lane = iota((128, 256), 1)
    b_out, c_out, d_out = dst_lane >> 6, (dst_lane >> 5) & 1, dst_lane & 31
    for d in range(4):
        want = ((c_out + 2 * odd) * 4 + b_out) * 8 + (d_out & 7)
        choose = jnp.logical_and(src_lane == want, (d_out >> 3) == d).astype(F32)
        result = result + dot(CO[d * 8:(d + 1) * 8].reshape(8, 128), choose)
    core_ref[...] = result

    for n in range(4):
        for up in (0, 1):
            @pl.when(has(("x", up)))
            def _():
                copy_x(n, up).wait_send()

            @pl.when(has(("y", up)))
            def _():
                for c in range(CHUNKS):
                    copy_y(n, up, c).wait_send()
    for c in range(CHUNKS):
        save(c).wait()
        spill(c).wait()


def body(v, flow, temp, diff, pre, energy, prod, east, north, vert, comp):
    vmem = pl.BlockSpec(memory_space=pltpu.VMEM)
    smem = pl.BlockSpec(memory_space=pltpu.SMEM)
    anywhere = pl.BlockSpec(memory_space=pl.ANY)
    field = (SPECIES, NX, NY, NZ)
    dma = pltpu.SemaphoreType.DMA
    tiles = lambda n: pltpu.VMEM((n, 8, 128), F32)
    final, resid, core = pl.pallas_call(
        kernel,
        out_shape=(
            jax.ShapeDtypeStruct(field, F32),
            jax.ShapeDtypeStruct(field, F32),
            jax.ShapeDtypeStruct((8, 256), F32),
        ),
        in_specs=[anywhere] * 3 + [smem] * 5 + [vmem] * 3,
        out_specs=(anywhere, anywhere, vmem),
        scratch_shapes=[
            pltpu.VMEM((5, SPECIES, NX + 2, NY, NZ), F32),
            pltpu.VMEM((3, NX, NY, NZ), F32),
            pltpu.VMEM((NX, NY, NZ), F32),
            pltpu.VMEM(field, F32),
            tiles(SPECIES * SPECIES),
            tiles(SPECIES * RANK_S),
            pltpu.VMEM((4, 2, NX, SPECIES, NZ), F32),
            pltpu.VMEM((4, 2, NX, SPECIES, NZ), F32),
            pltpu.VMEM((RANK_S, NX, NY, NZ), F32),
            pltpu.VMEM((NZ, 512), F32),
            tiles(DY),
            pltpu.VMEM((DX, NX, 128), F32),
            tiles(DY),
            tiles(DY),
            tiles(DX),
            tiles(DX),
            tiles(DX),
            tiles(DX),
            tiles(DY),
            tiles(DY),
            pltpu.VMEM((DX, 1, 128), F32),
            pltpu.VMEM((DY, 1, 128), F32),
            pltpu.VMEM(field, F32),
            dma((3,)),
            dma((2 * CHUNKS,)),
            dma((4, 2)), dma((4, 2)), dma((4, 2, CHUNKS)), dma((4, 2, CHUNKS)),
        ] + [dma] * 18,
        compiler_params=pltpu.CompilerParams(
            collective_id=0, has_side_effects=True, vmem_limit_bytes=48 << 20),
        name="flow_tucker",
    )(v, flow, temp, diff, pre, energy, prod, comp, east, north, vert)
    return final, resid, core.reshape(8, 4, 2, 32)


def solution(mesh):
    rows = ("gy", "ga")
    field = P(None, "gx", rows, None)
    in_specs = (
        field, field, P("gx", rows, None), P(), P(), P(), P(),
        P("gx", None), P(rows, None), P(), P(),
    )
    return jax.shard_map(
        body, mesh=mesh, in_specs=in_specs, out_specs=(field, field, field), check_vma=False)
```

```python
import functools
import jax
import jax.numpy as jnp
from jax import lax
from jax.experimental import pallas as pl
from jax.experimental.pallas import tpu as pltpu
from jax.sharding import PartitionSpec as P

MESH = pl.DeviceIdType.MESH
HI = lax.Precision.HIGHEST
F32 = jnp.float32
SPECIES = 16
RANK_S = 8
NX = 16
NY = 8
NZ = 128
DX = 16
DY = 32
GA = 4
GY = 8
ZL = 4
CHUNKS = 4
CX = NX // CHUNKS
ORDER = (0, 3, 1, 2)
EARLY, LATE = ORDER[:CHUNKS // 2], ORDER[CHUNKS // 2:]


def dot(a, b):
    return lax.dot_general(a, b, (((1,), (0,)), ((), ())), precision=HI, preferred_element_type=F32)


def dot_tn(a, b):
    return lax.dot_general(a, b, (((0,), (0,)), ((), ())), precision=HI, preferred_element_type=F32)


def dot_nt(a, b):
    return lax.dot_general(a, b, (((1,), (1,)), ((), ())), precision=HI, preferred_element_type=F32)


def iota(shape, dim):
    return lax.broadcasted_iota(jnp.int32, shape, dim)


def kernel(
    v_hbm, flow_hbm, temp_hbm, diff_ref, pre_ref, energy_ref, prod_ref, comp_ref,
    east_hbm, north_hbm, vert_hbm,
    final_ref, snap_ref, rec_ref, core_ref,
    V, F, T, K, PC, CC, HY, FY, S, VT, NF, EF,
    PB, G, QB, H, MB, Q8, UB, W, CS, CO, east_ref, north_ref, vert_ref,
    load_sem, out_sem,
    sx, rx, sy, ry,
    sn1, rn1, sn2, rn2, se1, re1, se2, re2,
    sp, rp, sq, rq, sm, rm, su, ru, sc, rc,
):
    gx = lax.axis_index("gx")
    gy = lax.axis_index("gy")
    ga = lax.axis_index("ga")
    me = gy * GA + ga
    zl = lax.rem(gx, ZL)
    xh = gx // ZL

    def at_y(j):
        return {"gx": gx, "gy": j // GA, "ga": lax.rem(j, GA)}

    def at_x(m):
        return {"gx": m, "gy": gy, "ga": ga}

    barrier = pltpu.get_barrier_semaphore()

    def greet_y(k, c):
        pl.semaphore_signal(barrier, inc=1, device_id=at_y(lax.rem(me + k, DY)), device_id_type=MESH)
        return c

    def greet_x(k, c):
        pl.semaphore_signal(barrier, inc=1, device_id=at_x(lax.rem(gx + k, DX)), device_id_type=MESH)
        return c

    lax.fori_loop(1, DY, greet_y, 0)
    lax.fori_loop(1, DX, greet_x, 0)

    load_v = pltpu.make_async_copy(v_hbm, V.at[0, :, pl.ds(1, NX)], load_sem.at[0])
    load_f = pltpu.make_async_copy(flow_hbm, F, load_sem.at[1])
    load_t = pltpu.make_async_copy(temp_hbm, T, load_sem.at[2])
    small = [
        pltpu.make_async_copy(east_hbm, east_ref, load_sem.at[3]),
        pltpu.make_async_copy(north_hbm, north_ref, load_sem.at[4]),
        pltpu.make_async_copy(vert_hbm, vert_ref, load_sem.at[5]),
    ]
    load_v.start()
    for load in [load_f, load_t] + small:
        load.start()

    zeros = jnp.zeros((SPECIES, NY, NZ), F32)
    zface = jnp.zeros((NX, SPECIES, NZ), F32)
    for n in range(4):
        @pl.when(gx == 0)
        def _():
            V[n, :, 0] = zeros

        @pl.when(gx == DX - 1)
        def _():
            V[n, :, NX + 1] = zeros

        @pl.when(me == 0)
        def _():
            HY[n, 0] = zface

        @pl.when(me == DY - 1)
        def _():
            HY[n, 1] = zface

    load_v.wait()

    def pack(x, c):
        for s in range(SPECIES):
            tile = V[0, s, x + 1]
            FY[0, 0, x, s:s + 1, :] = tile[0:1, :]
            FY[0, 1, x, s:s + 1, :] = tile[NY - 1:NY, :]
        return c

    lax.fori_loop(0, NX, pack, 0)
    pl.semaphore_wait(barrier, DY - 1 + DX - 1)

    def copy_x(n, up):
        return pltpu.make_async_remote_copy(
            src_ref=V.at[n, :, NX if up else 1],
            dst_ref=V.at[n, :, 0 if up else NX + 1],
            send_sem=sx.at[n, up],
            recv_sem=rx.at[n, up],
            device_id=at_x(gx + 1 if up else gx - 1),
            device_id_type=MESH,
        )

    def copy_y(n, up, c):
        part = pl.ds(c * CX, CX)
        return pltpu.make_async_remote_copy(
            src_ref=FY.at[n, up, part],
            dst_ref=HY.at[n, 1 - up, part],
            send_sem=sy.at[n, up, c],
            recv_sem=ry.at[n, up, c],
            device_id=at_y(me + 1 if up else me - 1),
            device_id_type=MESH,
        )

    def has(axis_up):
        axis, up = axis_up
        if axis == "x":
            return gx < DX - 1 if up else gx > 0
        return me < DY - 1 if up else me > 0

    def send_x(n, up):
        @pl.when(has(("x", up)))
        def _():
            copy_x(n, up).start()

    def send_y(n, c):
        for up in (0, 1):
            @pl.when(has(("y", up)))
            def _():
                copy_y(n, up, c).start()

    def recv_x(n, up):
        @pl.when(has(("x", 1 - up)))
        def _():
            copy_x(n, up).wait_recv()

    def recv_y(n, c):
        for up in (0, 1):
            @pl.when(has(("y", 1 - up)))
            def _():
                copy_y(n, up, c).wait_recv()

    send_x(0, 0)
    send_x(0, 1)
    for c in ORDER:
        send_y(0, c)

    for load in small:
        load.wait()
    old = iota((64, 128), 0)
    spread = (iota((64, 128), 1) == (old >> 2) * 8 + (old & 3)).astype(F32)
    NF[me] = dot(north_ref[...], spread)
    eye = (iota((64, 128), 1) == iota((64, 128), 0)).astype(F32)
    EF[gx] = dot(east_ref[...], eye)

    def n1(k):
        return pltpu.make_async_remote_copy(
            NF.at[me], NF.at[me], sn1, rn1,
            device_id=at_y(gy * GA + lax.rem(ga + k, GA)), device_id_type=MESH)

    def n2(k):
        part = pl.ds(gy * GA, GA)
        return pltpu.make_async_remote_copy(
            NF.at[part], NF.at[part], sn2, rn2,
            device_id=at_y(lax.rem(gy + k, GY) * GA + ga), device_id_type=MESH)

    def e1(k):
        return pltpu.make_async_remote_copy(
            EF.at[gx], EF.at[gx], se1, re1,
            device_id=at_x(xh * ZL + lax.rem(zl + k, ZL)), device_id_type=MESH)

    def e2(k):
        part = pl.ds(xh * ZL, ZL)
        return pltpu.make_async_remote_copy(
            EF.at[part], EF.at[part], se2, re2,
            device_id=at_x(lax.rem(xh + k, DX // ZL) * ZL + zl), device_id_type=MESH)

    for k in range(1, GA):
        n1(k).start()
    for k in range(1, ZL):
        e1(k).start()

    def taken(ref, send, recv):
        return pltpu.make_async_remote_copy(
            ref, ref, send, recv, device_id=at_y(lax.rem(me + 1, DY)), device_id_type=MESH)

    load_t.wait()
    load_f.wait()

    def rates(x, c):
        inverse = 1.0 / T[x]
        for k in range(SPECIES):
            K[k, x] = (0.5 * pre_ref[k]) * jnp.exp((-energy_ref[k]) * inverse)
        for d in range(3):
            F[d, x] = 0.25 * F[d, x]
        return c

    lax.fori_loop(0, NX, rates, 0)

    def splat(s, c):
        for k in range(SPECIES):
            PC[s * SPECIES + k] = jnp.full((8, 128), prod_ref[s, k], F32)
        for a in range(RANK_S):
            CC[s * RANK_S + a] = jnp.full((8, 128), comp_ref[a, s], F32)
        return c

    lax.fori_loop(0, SPECIES, splat, 0)

    spot = iota((32, 512), 1)
    pick = (iota((32, 512), 0) == (spot >> 7) * 8 + (spot & 7)).astype(F32)
    VT[...] = dot_tn(vert_ref[...], pick)

    row = iota((NY, NZ), 0)
    lane = iota((NY, NZ), 1)

    def advance(n, x, last):
        vs = [V[n, s, x + 1] for s in range(SPECIES)]
        react = [K[k, x] * vs[k] * vs[(k + 1) % SPECIES] for k in range(SPECIES)]
        fx, fy, fz = F[0, x], F[1, x], F[2, x]
        for s in range(SPECIES):
            v = vs[s]
            xp, xm = V[n, s, x + 2], V[n, s, x]
            up = jnp.broadcast_to(HY[n, 1, x, s:s + 1, :], (NY, NZ))
            down = jnp.broadcast_to(HY[n, 0, x, s:s + 1, :], (NY, NZ))
            yp = jnp.where(row == NY - 1, up, pltpu.roll(v, NY - 1, 0))
            ym = jnp.where(row == 0, down, pltpu.roll(v, 1, 0))
            zp = jnp.where(lane == NZ - 1, 0.0, pltpu.roll(v, NZ - 1, 1))
            zm = jnp.where(lane == 0, 0.0, pltpu.roll(v, 1, 1))
            half = 0.5 * diff_ref[s]
            total = (1.0 - 6.0 * half) * v + half * ((xp + xm) + (yp + ym) + (zp + zm))
            total = total - (fx * (xp - xm) + fy * (yp - ym) + fz * (zp - zm))
            made = PC[s * SPECIES] * react[0]
            for k in range(1, SPECIES):
                made = made + PC[s * SPECIES + k] * react[k]
            total = total + made
            V[n + 1, s, x + 1] = total
            if not last:
                FY[n + 1, 0, x, s:s + 1, :] = total[0:1, :]
                FY[n + 1, 1, x, s:s + 1, :] = total[NY - 1:NY, :]

    def step(n, c, send=True):
        last = n == 3
        recv_y(n, c)
        if c == 0:
            recv_x(n, 1)
        if c == CHUNKS - 1:
            recv_x(n, 0)

        def body(i, carry):
            advance(n, c * CX + i, last)
            return carry

        lax.fori_loop(0, CX, body, 0)
        if not last:
            if send:
                send_y(n + 1, c)
            if c == 0:
                send_x(n + 1, 0)
            if c == CHUNKS - 1:
                send_x(n + 1, 1)
        else:
            save(c).start()

    def save(c):
        return pltpu.make_async_copy(
            V.at[4, :, pl.ds(1 + c * CX, CX)],
            final_ref.at[:, pl.ds(c * CX, CX)],
            out_sem.at[c])

    step(0, ORDER[0])
    taken(NF.at[pl.ds(0, GA - 1)], sn1, rn1).wait()
    for k in range(1, GY):
        n2(k).start()
    taken(EF.at[pl.ds(0, ZL - 1)], se1, re1).wait()
    for k in range(1, DX // ZL):
        e2(k).start()
    for c in ORDER[1:]:
        step(0, c)
    def squash(x, carry):
        vs = [V[2, s, x + 1] for s in range(SPECIES)]
        for a in range(RANK_S):
            total = CC[a] * vs[0]
            for s in range(1, SPECIES):
                total = total + CC[s * RANK_S + a] * vs[s]
            S[a, x] = total
        return carry

    def project(c):
        where = ((iota((CX, NY, 512), 2) & 127) >> 3) == iota((CX, NY, 512), 0) + c * CX
        part = pl.ds(c * CX, CX)

        def one(a, carry):
            out = dot(S[a, part].reshape(CX * NY, NZ), VT[...]).reshape(CX, NY, 512)
            out = jnp.sum(jnp.where(where, out, 0.0), axis=0)
            for d in range(4):
                tile = out[:, d * 128:(d + 1) * 128]
                PB[a * 4 + d] = tile if c == ORDER[0] else PB[a * 4 + d] + tile
            return carry

        lax.fori_loop(0, RANK_S, one, 0)

    for c in ORDER:
        step(1, c, send=c in EARLY)
        lax.fori_loop(c * CX, (c + 1) * CX, squash, 0)
        project(c)

    def each_y(start):
        for g in (2, 1, 3, 0):
            def go(o, carry, g=g):
                start(lax.rem(gy + o, GY) * GA + lax.rem(ga + g, GA))
                return carry
            lax.fori_loop(0 if g else 1, GY, go, 0)

    def to_y(src, dst, send, recv):
        def start(j):
            pltpu.make_async_remote_copy(
                src.at[j], dst.at[me], send, recv, device_id=at_y(j), device_id_type=MESH).start()
        each_y(start)

    def to_x(src, dst, send, recv):
        for g in (2, 1, 3, 0):
            def go(o, carry, g=g):
                m = lax.rem(xh + g, DX // ZL) * ZL + lax.rem(zl + o, ZL)
                pltpu.make_async_remote_copy(
                    src.at[m], dst.at[gx], send, recv, device_id=at_x(m), device_id_type=MESH).start()
                return carry
            lax.fori_loop(0 if g else 1, ZL, go, 0)

    def done_y(ref, send, recv):
        taken(ref.at[pl.ds(0, DY - 1)], send, recv).wait()

    def done_x(ref, send, recv):
        taken(ref.at[pl.ds(0, DX - 1)], send, recv).wait()

    to_y(PB, G, sp, rp)
    G[me] = PB[me]
    keep = pltpu.make_async_copy(V.at[2, :, pl.ds(1, NX)], snap_ref, out_sem.at[CHUNKS])
    keep.start()
    for c in LATE:
        send_y(2, c)
    for c in EARLY:
        step(2, c, send=False)

    taken(NF.at[pl.ds(0, GA * (GY - 1))], sn2, rn2).wait()
    taken(EF.at[pl.ds(0, ZL * (DX // ZL - 1))], se2, re2).wait()
    done_y(G, sp, rp)
    north = NF[...].reshape(DY * NY, 128)
    QB[...] = dot_tn(north, G[...].reshape(DY * NY, 128)).reshape(DX, 8, 128)
    to_x(QB, H, sq, rq)
    H[gx] = QB[gx]
    for c in EARLY:
        send_y(3, c)
    for c in LATE:
        step(2, c, send=False)

    done_x(H, sq, rq)
    own_x = (iota((DX, NX, 128), 2) >> 3) == iota((DX, NX, 128), 1)
    blocks = []
    for c in range(4):
        spread_h = jnp.broadcast_to(H[:, c:c + 1, :], (DX, NX, 128))
        blocks.append(jnp.where(own_x, spread_h, 0.0).reshape(DX * NX, 128))
    east = EF[...].reshape(DX * NX, 128)
    core = dot_tn(east, jnp.concatenate(blocks, axis=1))
    piece = jnp.zeros((128, 128), F32)
    slot = iota((128, 128), 1) >> 3
    b_low = iota((128, 128), 0) & 3
    parts = []
    for c in range(4):
        part = core[:, c * 128:(c + 1) * 128]
        for shift in (64, 32, 16, 8):
            part = part + pltpu.roll(part, shift, 1)
        parts.append(part)
        piece = piece + jnp.where(slot == c * 4 + b_low, part, 0.0)
    out = dot(east, jnp.concatenate(parts, axis=1))
    for c in range(4):
        block = out[:, c * 128:(c + 1) * 128].reshape(DX, NX, 128)
        MB[:, c, :] = jnp.sum(jnp.where(own_x, block, 0.0), axis=1)
    MB[:, 4, :] = jnp.sum(piece[:64].reshape(DX, 4, 128), axis=1)
    for c in range(5, 8):
        MB[:, c, :] = jnp.zeros((DX, 128), F32)
    to_x(MB, Q8, sm, rm)
    Q8[gx] = MB[gx]
    for c in LATE:
        send_y(3, c)
    step(3, ORDER[0])

    done_x(Q8, sm, rm)
    UB[...] = dot(NF[...].reshape(DY * NY, 128), Q8[...].reshape(DX * 8, 128)).reshape(DY, NY, 128)
    to_y(UB, W, su, ru)
    W[me] = UB[me]
    for m in range(DX):
        CS[m] = Q8[m, 4:5, :]
    own = CO.at[lax.rem(me, 4) * 8 + me // 4]

    def core_go(j):
        pltpu.make_async_remote_copy(
            CS.at[j // 2], own, sc, rc, device_id=at_y(j), device_id_type=MESH).start()

    each_y(core_go)
    CO[lax.rem(me, 4) * 8 + me // 4] = CS[me // 2]

    for c in ORDER[1:]:
        step(3, c)

    done_y(W, su, ru)
    tall = (iota((NX, NY, 128), 2) >> 3) == iota((NX, NY, 128), 0)

    def rebuild(a, carry):
        left = []
        for d in range(4):
            copies = jnp.broadcast_to(W[a * 4 + d][None], (NX, NY, 128))
            left.append(jnp.where(tall, copies, 0.0).reshape(NX * NY, 128))
        rec_ref[a] = dot_nt(jnp.concatenate(left, axis=1), VT[...]).reshape(NX, NY, NZ)
        return carry

    lax.fori_loop(0, RANK_S, rebuild, 0)

    taken(CO.at[pl.ds(0, DY - 1)], sc, rc).wait()
    odd = lax.rem(me, 2)
    result = jnp.zeros((8, 256), F32)
    src_lane = iota((128, 256), 0)
    dst_lane = iota((128, 256), 1)
    b_out, c_out, d_out = dst_lane >> 6, (dst_lane >> 5) & 1, dst_lane & 31
    for d in range(4):
        want = ((c_out + 2 * odd) * 4 + b_out) * 8 + (d_out & 7)
        choose = jnp.logical_and(src_lane == want, (d_out >> 3) == d).astype(F32)
        result = result + dot(CO[d * 8:(d + 1) * 8].reshape(8, 128), choose)
    for i in range(8):
        core_ref[i] = result[:, i * 32:(i + 1) * 32]

    for n in range(4):
        for up in (0, 1):
            @pl.when(has(("x", up)))
            def _():
                copy_x(n, up).wait_send()

            @pl.when(has(("y", up)))
            def _():
                for c in range(CHUNKS):
                    copy_y(n, up, c).wait_send()
    for c in range(CHUNKS):
        save(c).wait()
    keep.wait()


def finish(final_ref, snap_ref, rec_ref, comp_ref, final_hbm, resid_hbm, RES, sem):
    out = pltpu.make_async_copy(final_ref, final_hbm, sem.at[CHUNKS])
    out.start()

    def spill(c):
        return pltpu.make_async_copy(
            RES.at[:, pl.ds(c * CX, CX)], resid_hbm.at[:, pl.ds(c * CX, CX)], sem.at[c])

    def subtract(x, carry):
        rs = [rec_ref[a, x] for a in range(RANK_S)]
        for s in range(SPECIES):
            total = snap_ref[s, x]
            for a in range(RANK_S):
                total = total - comp_ref[a, s] * rs[a]
            RES[s, x] = total
        return carry

    for c in range(CHUNKS):
        lax.fori_loop(c * CX, (c + 1) * CX, subtract, 0)
        spill(c).start()
    for c in range(CHUNKS):
        spill(c).wait()
    out.wait()


def body(v, flow, temp, diff, pre, energy, prod, east, north, vert, comp):
    vmem = pl.BlockSpec(memory_space=pltpu.VMEM)
    hbm = pl.BlockSpec(memory_space=pltpu.HBM)
    smem = pl.BlockSpec(memory_space=pltpu.SMEM)
    field = (SPECIES, NX, NY, NZ)
    dma = pltpu.SemaphoreType.DMA
    tiles = lambda n: pltpu.VMEM((n, 8, 128), F32)
    comp_t = comp.T
    v, flow, temp, east, north, vert, diff, pre, energy, prod, comp = [
        pltpu.with_memory_space_constraint(a, pltpu.HBM)
        for a in (v, flow, temp, east, north, vert.T, diff, pre, energy, prod, comp_t)]
    final, snap, rec, core = pl.pallas_call(
        kernel,
        out_shape=(
            jax.ShapeDtypeStruct(field, F32),
            jax.ShapeDtypeStruct(field, F32),
            jax.ShapeDtypeStruct((RANK_S, NX, NY, NZ), F32),
            jax.ShapeDtypeStruct((8, 8, 32), F32),
        ),
        in_specs=[hbm] * 3 + [smem] * 5 + [hbm] * 3,
        out_specs=(vmem,) * 4,
        scratch_shapes=[
            pltpu.VMEM((5, SPECIES, NX + 2, NY, NZ), F32),
            pltpu.VMEM((3, NX, NY, NZ), F32),
            pltpu.VMEM((NX, NY, NZ), F32),
            pltpu.VMEM(field, F32),
            tiles(SPECIES * SPECIES),
            tiles(SPECIES * RANK_S),
            pltpu.VMEM((4, 2, NX, SPECIES, NZ), F32),
            pltpu.VMEM((4, 2, NX, SPECIES, NZ), F32),
            pltpu.VMEM((RANK_S, NX, NY, NZ), F32),
            pltpu.VMEM((NZ, 512), F32),
            tiles(DY),
            pltpu.VMEM((DX, NX, 128), F32),
            tiles(DY),
            tiles(DY),
            tiles(DX),
            tiles(DX),
            tiles(DX),
            tiles(DX),
            tiles(DY),
            tiles(DY),
            pltpu.VMEM((DX, 1, 128), F32),
            pltpu.VMEM((DY, 1, 128), F32),
            pltpu.VMEM((NX, 64), F32), pltpu.VMEM((NY, 64), F32), pltpu.VMEM((32, NZ), F32),
            dma((6,)),
            dma((2 * CHUNKS,)),
            dma((4, 2)), dma((4, 2)), dma((4, 2, CHUNKS)), dma((4, 2, CHUNKS)),
        ] + [dma] * 18,
        compiler_params=pltpu.CompilerParams(
            collective_id=0, has_side_effects=True, vmem_limit_bytes=48 << 20),
        name="flow_tucker",
    )(v, flow, temp, diff, pre, energy, prod, comp, east, north, vert)
    final, resid = pl.pallas_call(
        finish,
        out_shape=(jax.ShapeDtypeStruct(field, F32),) * 2,
        in_specs=[vmem] * 3 + [smem],
        out_specs=(hbm, hbm),
        scratch_shapes=[pltpu.VMEM(field, F32), dma((CHUNKS + 1,))],
        compiler_params=pltpu.CompilerParams(vmem_limit_bytes=16 << 20),
        name="finish",
    )(final, snap, rec, comp)
    return final, resid, core.transpose(1, 0, 2).reshape(8, 4, 2, 32)


def solution(mesh):
    rows = ("gy", "ga")
    field = P(None, "gx", rows, None)
    in_specs = (
        field, field, P("gx", rows, None), P(), P(), P(), P(),
        P("gx", None), P(rows, None), P(), P(),
    )
    return jax.shard_map(
        body, mesh=mesh, in_specs=in_specs, out_specs=(field, field, field), check_vma=False)
```

```python
import functools
import jax
import jax.numpy as jnp
from jax import lax
from jax.experimental import pallas as pl
from jax.experimental.pallas import tpu as pltpu
from jax.sharding import PartitionSpec as P

MESH = pl.DeviceIdType.MESH
HI = lax.Precision.HIGHEST
F32 = jnp.float32
SPECIES = 16
RANK_S = 8
NX = 16
NY = 8
NZ = 128
DX = 16
DY = 32
GA = 4
GY = 8
ZL = 4
CHUNKS = 4
CX = NX // CHUNKS
ORDER = (0, 3, 1, 2)
EARLY, LATE = ORDER[:CHUNKS // 2], ORDER[CHUNKS // 2:]


def dot(a, b):
    return lax.dot_general(a, b, (((1,), (0,)), ((), ())), precision=HI, preferred_element_type=F32)


def dot_tn(a, b):
    return lax.dot_general(a, b, (((0,), (0,)), ((), ())), precision=HI, preferred_element_type=F32)


def dot_nt(a, b):
    return lax.dot_general(a, b, (((1,), (1,)), ((), ())), precision=HI, preferred_element_type=F32)


def iota(shape, dim):
    return lax.broadcasted_iota(jnp.int32, shape, dim)


def kernel(
    v_hbm, flow_hbm, temp_hbm, diff_ref, pre_ref, energy_ref, prod_ref, comp_ref,
    east_hbm, north_hbm, vert_hbm,
    final_ref, snap_ref, rec_ref, core_ref,
    V, F, T, K, PC, CC, HY, FY, S, VT, NF, EF,
    PB, G, QB, H, MB, Q8, UB, W, CS, CO, QS, east_ref, north_ref, vert_ref,
    load_sem, out_sem,
    sx, rx, sy, ry,
    sn1, rn1, sn2, rn2, se1, re1, se2, re2,
    sp, rp, sq, rq, sm, rm, su, ru, sc, rc,
):
    gx = lax.axis_index("gx")
    gy = lax.axis_index("gy")
    ga = lax.axis_index("ga")
    me = gy * GA + ga
    zl = lax.rem(gx, ZL)
    xh = gx // ZL

    def at_y(j):
        return {"gx": gx, "gy": j // GA, "ga": lax.rem(j, GA)}

    def at_x(m):
        return {"gx": m, "gy": gy, "ga": ga}

    barrier = pltpu.get_barrier_semaphore()

    def greet_y(k, c):
        pl.semaphore_signal(barrier, inc=1, device_id=at_y(lax.rem(me + k, DY)), device_id_type=MESH)
        return c

    def greet_x(k, c):
        pl.semaphore_signal(barrier, inc=1, device_id=at_x(lax.rem(gx + k, DX)), device_id_type=MESH)
        return c

    lax.fori_loop(1, DY, greet_y, 0)
    lax.fori_loop(1, DX, greet_x, 0)

    load_v = pltpu.make_async_copy(v_hbm, V.at[0, :, pl.ds(1, NX)], load_sem.at[0])
    load_f = pltpu.make_async_copy(flow_hbm, F, load_sem.at[1])
    load_t = pltpu.make_async_copy(temp_hbm, T, load_sem.at[2])
    small = [
        pltpu.make_async_copy(east_hbm, east_ref, load_sem.at[3]),
        pltpu.make_async_copy(north_hbm, north_ref, load_sem.at[4]),
        pltpu.make_async_copy(vert_hbm, vert_ref, load_sem.at[5]),
    ]
    load_v.start()
    for load in [load_f, load_t] + small:
        load.start()

    zeros = jnp.zeros((SPECIES, NY, NZ), F32)
    zface = jnp.zeros((NX, SPECIES, NZ), F32)
    for n in range(4):
        @pl.when(gx == 0)
        def _():
            V[n, :, 0] = zeros

        @pl.when(gx == DX - 1)
        def _():
            V[n, :, NX + 1] = zeros

        @pl.when(me == 0)
        def _():
            HY[n, 0] = zface

        @pl.when(me == DY - 1)
        def _():
            HY[n, 1] = zface

    load_v.wait()

    def pack(x, c):
        for s in range(SPECIES):
            tile = V[0, s, x + 1]
            FY[0, 0, x, s:s + 1, :] = tile[0:1, :]
            FY[0, 1, x, s:s + 1, :] = tile[NY - 1:NY, :]
        return c

    lax.fori_loop(0, NX, pack, 0)
    pl.semaphore_wait(barrier, DY - 1 + DX - 1)

    def copy_x(n, up):
        return pltpu.make_async_remote_copy(
            src_ref=V.at[n, :, NX if up else 1],
            dst_ref=V.at[n, :, 0 if up else NX + 1],
            send_sem=sx.at[n, up],
            recv_sem=rx.at[n, up],
            device_id=at_x(gx + 1 if up else gx - 1),
            device_id_type=MESH,
        )

    def copy_y(n, up, c):
        part = pl.ds(c * CX, CX)
        return pltpu.make_async_remote_copy(
            src_ref=FY.at[n, up, part],
            dst_ref=HY.at[n, 1 - up, part],
            send_sem=sy.at[n, up, c],
            recv_sem=ry.at[n, up, c],
            device_id=at_y(me + 1 if up else me - 1),
            device_id_type=MESH,
        )

    def has(axis_up):
        axis, up = axis_up
        if axis == "x":
            return gx < DX - 1 if up else gx > 0
        return me < DY - 1 if up else me > 0

    def send_x(n, up):
        @pl.when(has(("x", up)))
        def _():
            copy_x(n, up).start()

    def send_y(n, c):
        for up in (0, 1):
            @pl.when(has(("y", up)))
            def _():
                copy_y(n, up, c).start()

    def recv_x(n, up):
        @pl.when(has(("x", 1 - up)))
        def _():
            copy_x(n, up).wait_recv()

    def recv_y(n, c):
        for up in (0, 1):
            @pl.when(has(("y", 1 - up)))
            def _():
                copy_y(n, up, c).wait_recv()

    send_x(0, 0)
    send_x(0, 1)
    for c in ORDER:
        send_y(0, c)

    for load in small:
        load.wait()
    eye = (iota((64, 128), 1) == iota((64, 128), 0)).astype(F32)
    NF[me] = dot(north_ref[...], eye)
    EF[gx] = dot(east_ref[...], eye)

    def n1(k):
        return pltpu.make_async_remote_copy(
            NF.at[me], NF.at[me], sn1, rn1,
            device_id=at_y(gy * GA + lax.rem(ga + k, GA)), device_id_type=MESH)

    def n2(k):
        part = pl.ds(gy * GA, GA)
        return pltpu.make_async_remote_copy(
            NF.at[part], NF.at[part], sn2, rn2,
            device_id=at_y(lax.rem(gy + k, GY) * GA + ga), device_id_type=MESH)

    def e1(k):
        return pltpu.make_async_remote_copy(
            EF.at[gx], EF.at[gx], se1, re1,
            device_id=at_x(xh * ZL + lax.rem(zl + k, ZL)), device_id_type=MESH)

    def e2(k):
        part = pl.ds(xh * ZL, ZL)
        return pltpu.make_async_remote_copy(
            EF.at[part], EF.at[part], se2, re2,
            device_id=at_x(lax.rem(xh + k, DX // ZL) * ZL + zl), device_id_type=MESH)

    for k in range(1, GA):
        n1(k).start()
    for k in range(1, ZL):
        e1(k).start()

    def taken(ref, send, recv):
        return pltpu.make_async_remote_copy(
            ref, ref, send, recv, device_id=at_y(lax.rem(me + 1, DY)), device_id_type=MESH)

    load_t.wait()
    load_f.wait()

    def rates(x, c):
        inverse = 1.0 / T[x]
        for k in range(SPECIES):
            K[k, x] = (0.5 * pre_ref[k]) * jnp.exp((-energy_ref[k]) * inverse)
        for d in range(3):
            F[d, x] = 0.25 * F[d, x]
        return c

    lax.fori_loop(0, NX, rates, 0)

    def splat(s, c):
        for k in range(SPECIES):
            PC[s * SPECIES + k] = jnp.full((8, 128), prod_ref[s, k], F32)
        for a in range(RANK_S):
            CC[s * RANK_S + a] = jnp.full((8, 128), comp_ref[a, s], F32)
        return c

    lax.fori_loop(0, SPECIES, splat, 0)

    spot = iota((32, 256), 1)
    pick = (iota((32, 256), 0) == (spot >> 7) * 16 + (spot & 15)).astype(F32)
    VT[...] = dot_tn(vert_ref[...], pick)

    row = iota((NY, NZ), 0)
    lane = iota((NY, NZ), 1)

    def advance(n, x, last):
        vs = [V[n, s, x + 1] for s in range(SPECIES)]
        react = [K[k, x] * vs[k] * vs[(k + 1) % SPECIES] for k in range(SPECIES)]
        fx, fy, fz = F[0, x], F[1, x], F[2, x]
        for s in range(SPECIES):
            v = vs[s]
            xp, xm = V[n, s, x + 2], V[n, s, x]
            up = jnp.broadcast_to(HY[n, 1, x, s:s + 1, :], (NY, NZ))
            down = jnp.broadcast_to(HY[n, 0, x, s:s + 1, :], (NY, NZ))
            yp = jnp.where(row == NY - 1, up, pltpu.roll(v, NY - 1, 0))
            ym = jnp.where(row == 0, down, pltpu.roll(v, 1, 0))
            zp = jnp.where(lane == NZ - 1, 0.0, pltpu.roll(v, NZ - 1, 1))
            zm = jnp.where(lane == 0, 0.0, pltpu.roll(v, 1, 1))
            half = 0.5 * diff_ref[s]
            total = (1.0 - 6.0 * half) * v + half * ((xp + xm) + (yp + ym) + (zp + zm))
            total = total - (fx * (xp - xm) + fy * (yp - ym) + fz * (zp - zm))
            made = PC[s * SPECIES] * react[0]
            for k in range(1, SPECIES):
                made = made + PC[s * SPECIES + k] * react[k]
            total = total + made
            V[n + 1, s, x + 1] = total
            if not last:
                FY[n + 1, 0, x, s:s + 1, :] = total[0:1, :]
                FY[n + 1, 1, x, s:s + 1, :] = total[NY - 1:NY, :]

    def step(n, c, send=True):
        last = n == 3
        recv_y(n, c)
        if c == 0:
            recv_x(n, 1)
        if c == CHUNKS - 1:
            recv_x(n, 0)

        def body(i, carry):
            advance(n, c * CX + i, last)
            return carry

        lax.fori_loop(0, CX, body, 0)
        if not last:
            if send:
                send_y(n + 1, c)
            if c == 0:
                send_x(n + 1, 0)
            if c == CHUNKS - 1:
                send_x(n + 1, 1)
        else:
            save(c).start()

    def save(c):
        return pltpu.make_async_copy(
            V.at[4, :, pl.ds(1 + c * CX, CX)],
            final_ref.at[:, pl.ds(c * CX, CX)],
            out_sem.at[c])

    step(0, ORDER[0])
    taken(NF.at[pl.ds(0, GA - 1)], sn1, rn1).wait()
    for k in range(1, GY):
        n2(k).start()
    taken(EF.at[pl.ds(0, ZL - 1)], se1, re1).wait()
    for k in range(1, DX // ZL):
        e2(k).start()
    for c in ORDER[1:]:
        step(0, c)
    def squash(x, carry):
        vs = [V[2, s, x + 1] for s in range(SPECIES)]
        for a in range(RANK_S):
            total = CC[a] * vs[0]
            for s in range(1, SPECIES):
                total = total + CC[s * RANK_S + a] * vs[s]
            S[a, x] = total
        return carry

    def project(c):
        where = ((iota((CX, NY, 256), 2) & 127) >> 4) == iota((CX, NY, 256), 1)
        part = pl.ds(c * CX, CX)

        def one(a, carry):
            out = dot(S[a, part].reshape(CX * NY, NZ), VT[...]).reshape(CX, NY, 256)
            out = jnp.sum(jnp.where(where, out, 0.0), axis=1)
            for d in range(2):
                PB[a * 2 + d, c * CX:(c + 1) * CX, :] = out[:, d * 128:(d + 1) * 128]
            return carry

        lax.fori_loop(0, RANK_S, one, 0)

    for c in ORDER:
        step(1, c, send=c in EARLY)
        lax.fori_loop(c * CX, (c + 1) * CX, squash, 0)
        project(c)

    def each_y(start):
        for g in (2, 1, 3, 0):
            def go(o, carry, g=g):
                start(lax.rem(gy + o, GY) * GA + lax.rem(ga + g, GA))
                return carry
            lax.fori_loop(0 if g else 1, GY, go, 0)

    def to_y(src, dst, send, recv):
        def start(j):
            pltpu.make_async_remote_copy(
                src.at[j], dst.at[me], send, recv, device_id=at_y(j), device_id_type=MESH).start()
        each_y(start)

    def each_x(start):
        for g in (2, 1, 3, 0):
            def go(o, carry, g=g):
                start(lax.rem(xh + g, DX // ZL) * ZL + lax.rem(zl + o, ZL))
                return carry
            lax.fori_loop(0 if g else 1, ZL, go, 0)

    def to_x(src, dst, send, recv):
        def start(m):
            pltpu.make_async_remote_copy(
                src.at[m], dst.at[gx], send, recv, device_id=at_x(m), device_id_type=MESH).start()
        each_x(start)

    def done_y(ref, send, recv):
        taken(ref.at[pl.ds(0, DY - 1)], send, recv).wait()

    def done_x(ref, send, recv):
        taken(ref.at[pl.ds(0, DX - 1)], send, recv).wait()

    to_x(PB, G, sp, rp)
    G[gx] = PB[gx]
    keep = pltpu.make_async_copy(V.at[2, :, pl.ds(1, NX)], snap_ref, out_sem.at[CHUNKS])
    keep.start()
    for c in LATE:
        send_y(2, c)
    for c in EARLY:
        step(2, c, send=False)

    taken(NF.at[pl.ds(0, GA * (GY - 1))], sn2, rn2).wait()
    taken(EF.at[pl.ds(0, ZL * (DX // ZL - 1))], se2, re2).wait()
    done_x(G, sp, rp)
    east = EF[...].reshape(DX * NX, 128)
    pairs = dot_tn(east, G[...].reshape(DX * NX, 128))
    for j in range(DY):
        QB[j] = pairs[2 * j:2 * j + 2, :]
    to_y(QB, H, sq, rq)
    H[me] = QB[me]
    for c in EARLY:
        send_y(3, c)
    for c in LATE:
        step(2, c, send=False)

    done_y(H, sq, rq)
    own_y = (iota((DY, NY, 128), 2) >> 4) == iota((DY, NY, 128), 1)
    blocks = []
    for b in range(2):
        spread_h = jnp.broadcast_to(H[:, b:b + 1, :], (DY, NY, 128))
        blocks.append(jnp.where(own_y, spread_h, 0.0).reshape(DY * NY, 128))
    north = NF[...].reshape(DY * NY, 128)
    core = dot_tn(north, jnp.concatenate(blocks, axis=1))
    piece = jnp.zeros((128, 128), F32)
    slot = iota((128, 128), 1) >> 4
    c_low = iota((128, 128), 0) & 1
    parts = []
    for b in range(2):
        part = core[:, b * 128:(b + 1) * 128]
        for shift in (64, 32, 16):
            part = part + pltpu.roll(part, shift, 1)
        parts.append(part)
        piece = piece + jnp.where(slot == b * 2 + c_low, part, 0.0)
    out = dot(north, jnp.concatenate(parts, axis=1))
    for b in range(2):
        block = out[:, b * 128:(b + 1) * 128].reshape(DY, NY, 128)
        MB[:, b, :] = jnp.sum(jnp.where(own_y, block, 0.0), axis=1)
    MB[:, 2, :] = jnp.sum(piece[:64].reshape(DY, 2, 128), axis=1)
    MB[:, 3, :] = jnp.zeros((DY, 128), F32)
    to_y(MB, Q8, sm, rm)
    Q8[me] = MB[me]
    for c in LATE:
        send_y(3, c)
    step(3, ORDER[0])

    QS[64:, :] = jnp.zeros((64, 128), F32)
    done_y(Q8, sm, rm)
    for j in range(DY):
        QS[2 * j:2 * j + 2, :] = Q8[j, 0:2, :]
    UB[...] = dot(EF[...].reshape(DX * NX, 128), QS[...]).reshape(DX, NX, 128)
    to_x(UB, W, su, ru)
    W[gx] = UB[gx]
    for j in range(DY):
        CS[j // 2, j % 2] = Q8[j, 2:3, :]
    home = lax.rem(gx, 2) * 8 + gx // 2

    def core_go(m):
        pltpu.make_async_remote_copy(
            CS.at[m], CO.at[home], sc, rc, device_id=at_x(m), device_id_type=MESH).start()

    each_x(core_go)
    CO[home] = CS[gx]

    for c in ORDER[1:]:
        step(3, c)

    done_x(W, su, ru)
    own_row = (iota((NY, 128), 1) >> 4) == iota((NY, 128), 0)

    def rebuild(a, carry):
        left = []
        for d in range(2):
            rows = []
            for x in range(NX):
                copies = jnp.broadcast_to(W[a * 2 + d, x:x + 1, :], (NY, 128))
                rows.append(jnp.where(own_row, copies, 0.0))
            left.append(jnp.concatenate(rows, axis=0))
        rec_ref[a] = dot_nt(jnp.concatenate(left, axis=1), VT[...]).reshape(NX, NY, NZ)
        return carry

    lax.fori_loop(0, RANK_S, rebuild, 0)

    taken(CO.at[pl.ds(0, DX - 1)], sc, rc).wait()
    result = jnp.zeros((8, 256), F32)
    src_lane = iota((128, 256), 0)
    dst_lane = iota((128, 256), 1)
    b_out, c_out, d_out = dst_lane >> 6, (dst_lane >> 5) & 1, dst_lane & 31
    want = ((b_out & 1) * 2 + c_out) * 16 + (d_out & 15)
    for d in range(2):
        for b in range(2):
            here = jnp.logical_and((b_out >> 1) == b, (d_out >> 4) == d)
            choose = jnp.logical_and(src_lane == want, here).astype(F32)
            result = result + dot(CO[d * 8:(d + 1) * 8, b].reshape(8, 128), choose)
    for i in range(8):
        core_ref[i] = result[:, i * 32:(i + 1) * 32]

    for n in range(4):
        for up in (0, 1):
            @pl.when(has(("x", up)))
            def _():
                copy_x(n, up).wait_send()

            @pl.when(has(("y", up)))
            def _():
                for c in range(CHUNKS):
                    copy_y(n, up, c).wait_send()
    for c in range(CHUNKS):
        save(c).wait()
    keep.wait()


def finish(final_ref, snap_ref, rec_ref, comp_ref, final_hbm, resid_hbm, RES, sem):
    out = pltpu.make_async_copy(final_ref, final_hbm, sem.at[CHUNKS])
    out.start()

    def spill(c):
        return pltpu.make_async_copy(
            RES.at[:, pl.ds(c * CX, CX)], resid_hbm.at[:, pl.ds(c * CX, CX)], sem.at[c])

    def subtract(x, carry):
        rs = [rec_ref[a, x] for a in range(RANK_S)]
        for s in range(SPECIES):
            total = snap_ref[s, x]
            for a in range(RANK_S):
                total = total - comp_ref[a, s] * rs[a]
            RES[s, x] = total
        return carry

    for c in range(CHUNKS):
        lax.fori_loop(c * CX, (c + 1) * CX, subtract, 0)
        spill(c).start()
    for c in range(CHUNKS):
        spill(c).wait()
    out.wait()


def body(v, flow, temp, diff, pre, energy, prod, east, north, vert, comp):
    vmem = pl.BlockSpec(memory_space=pltpu.VMEM)
    hbm = pl.BlockSpec(memory_space=pltpu.HBM)
    smem = pl.BlockSpec(memory_space=pltpu.SMEM)
    field = (SPECIES, NX, NY, NZ)
    dma = pltpu.SemaphoreType.DMA
    tiles = lambda n: pltpu.VMEM((n, 8, 128), F32)
    comp_t = comp.T
    v, flow, temp, east, north, vert, diff, pre, energy, prod, comp = [
        pltpu.with_memory_space_constraint(a, pltpu.HBM)
        for a in (v, flow, temp, east, north, vert.T, diff, pre, energy, prod, comp_t)]
    final, snap, rec, core = pl.pallas_call(
        kernel,
        out_shape=(
            jax.ShapeDtypeStruct(field, F32),
            jax.ShapeDtypeStruct(field, F32),
            jax.ShapeDtypeStruct((RANK_S, NX, NY, NZ), F32),
            jax.ShapeDtypeStruct((8, 8, 32), F32),
        ),
        in_specs=[hbm] * 3 + [smem] * 5 + [hbm] * 3,
        out_specs=(vmem,) * 4,
        scratch_shapes=[
            pltpu.VMEM((5, SPECIES, NX + 2, NY, NZ), F32),
            pltpu.VMEM((3, NX, NY, NZ), F32),
            pltpu.VMEM((NX, NY, NZ), F32),
            pltpu.VMEM(field, F32),
            tiles(SPECIES * SPECIES),
            tiles(SPECIES * RANK_S),
            pltpu.VMEM((4, 2, NX, SPECIES, NZ), F32),
            pltpu.VMEM((4, 2, NX, SPECIES, NZ), F32),
            pltpu.VMEM((RANK_S, NX, NY, NZ), F32),
            pltpu.VMEM((NZ, 256), F32),
            tiles(DY),
            pltpu.VMEM((DX, NX, 128), F32),
            pltpu.VMEM((DX, NX, 128), F32),
            pltpu.VMEM((DX, NX, 128), F32),
            pltpu.VMEM((DY, 2, 128), F32),
            pltpu.VMEM((DY, 2, 128), F32),
            pltpu.VMEM((DY, 4, 128), F32),
            pltpu.VMEM((DY, 4, 128), F32),
            pltpu.VMEM((DX, NX, 128), F32),
            pltpu.VMEM((DX, NX, 128), F32),
            pltpu.VMEM((DX, 2, 1, 128), F32),
            pltpu.VMEM((DX, 2, 1, 128), F32),
            pltpu.VMEM((128, 128), F32),
            pltpu.VMEM((NX, 64), F32), pltpu.VMEM((NY, 64), F32), pltpu.VMEM((32, NZ), F32),
            dma((6,)),
            dma((2 * CHUNKS,)),
            dma((4, 2)), dma((4, 2)), dma((4, 2, CHUNKS)), dma((4, 2, CHUNKS)),
        ] + [dma] * 18,
        compiler_params=pltpu.CompilerParams(
            collective_id=0, has_side_effects=True, vmem_limit_bytes=48 << 20),
        name="flow_tucker",
    )(v, flow, temp, diff, pre, energy, prod, comp, east, north, vert)
    final, resid = pl.pallas_call(
        finish,
        out_shape=(jax.ShapeDtypeStruct(field, F32),) * 2,
        in_specs=[vmem] * 3 + [smem],
        out_specs=(hbm, hbm),
        scratch_shapes=[pltpu.VMEM(field, F32), dma((CHUNKS + 1,))],
        compiler_params=pltpu.CompilerParams(vmem_limit_bytes=16 << 20),
        name="finish",
    )(final, snap, rec, comp)
    return final, resid, core.transpose(1, 0, 2).reshape(8, 4, 2, 32)


def solution(mesh):
    rows = ("gy", "ga")
    field = P(None, "gx", rows, None)
    in_specs = (
        field, field, P("gx", rows, None), P(), P(), P(), P(),
        P("gx", None), P(rows, None), P(), P(),
    )
    return jax.shard_map(
        body, mesh=mesh, in_specs=in_specs, out_specs=(field, field, field), check_vma=False)
```

```python
import functools
import jax
import jax.numpy as jnp
from jax import lax
from jax.experimental import pallas as pl
from jax.experimental.pallas import tpu as pltpu
from jax.sharding import PartitionSpec as P

MESH = pl.DeviceIdType.MESH
HI = lax.Precision.HIGHEST
F32 = jnp.float32
SPECIES = 16
RANK_S = 8
NX = 16
NY = 8
NZ = 128
DX = 16
DY = 32
GA = 4
GY = 8
ZL = 4
CHUNKS = 4
CX = NX // CHUNKS
ORDER = (0, 3, 1, 2)
EARLY, LATE = ORDER[:CHUNKS // 2], ORDER[CHUNKS // 2:]


def dot(a, b):
    return lax.dot_general(a, b, (((1,), (0,)), ((), ())), precision=HI, preferred_element_type=F32)


def dot_tn(a, b):
    return lax.dot_general(a, b, (((0,), (0,)), ((), ())), precision=HI, preferred_element_type=F32)


def dot_nt(a, b):
    return lax.dot_general(a, b, (((1,), (1,)), ((), ())), precision=HI, preferred_element_type=F32)


def iota(shape, dim):
    return lax.broadcasted_iota(jnp.int32, shape, dim)


def kernel(
    v_hbm, flow_hbm, temp_hbm, diff_ref, pre_ref, energy_ref, prod_ref, comp_ref,
    east_hbm, north_hbm, vert_hbm,
    final_ref, snap_ref, rec_ref, core_ref,
    V, F, T, K, PC, CC, HY, FY, S, VT, NF, EF,
    PB, G, QB, H, MB, Q8, UB, W, CS, CO, QS, east_ref, north_ref, vert_ref,
    load_sem, out_sem,
    sx, rx, sy, ry,
    sn1, rn1, sn2, rn2, se1, re1, se2, re2,
    sp, rp, sq, rq, sm, rm, su, ru, sc, rc,
):
    gx = lax.axis_index("gx")
    gy = lax.axis_index("gy")
    ga = lax.axis_index("ga")
    me = gy * GA + ga
    zl = lax.rem(gx, ZL)
    xh = gx // ZL

    def at_y(j):
        return {"gx": gx, "gy": j // GA, "ga": lax.rem(j, GA)}

    def at_x(m):
        return {"gx": m, "gy": gy, "ga": ga}

    barrier = pltpu.get_barrier_semaphore()

    def greet_y(k, c):
        pl.semaphore_signal(barrier, inc=1, device_id=at_y(lax.rem(me + k, DY)), device_id_type=MESH)
        return c

    def greet_x(k, c):
        pl.semaphore_signal(barrier, inc=1, device_id=at_x(lax.rem(gx + k, DX)), device_id_type=MESH)
        return c

    lax.fori_loop(1, DY, greet_y, 0)
    lax.fori_loop(1, DX, greet_x, 0)

    load_v = pltpu.make_async_copy(v_hbm, V.at[0, :, pl.ds(1, NX)], load_sem.at[0])
    load_f = pltpu.make_async_copy(flow_hbm, F, load_sem.at[1])
    load_t = pltpu.make_async_copy(temp_hbm, T, load_sem.at[2])
    small = [
        pltpu.make_async_copy(east_hbm, east_ref, load_sem.at[3]),
        pltpu.make_async_copy(north_hbm, north_ref, load_sem.at[4]),
        pltpu.make_async_copy(vert_hbm, vert_ref, load_sem.at[5]),
    ]
    load_v.start()
    for load in [load_f, load_t] + small:
        load.start()

    zeros = jnp.zeros((SPECIES, NY, NZ), F32)
    zface = jnp.zeros((NX, SPECIES, NZ), F32)
    for n in range(4):
        @pl.when(gx == 0)
        def _():
            V[n, :, 0] = zeros

        @pl.when(gx == DX - 1)
        def _():
            V[n, :, NX + 1] = zeros

        @pl.when(me == 0)
        def _():
            HY[n, 0] = zface

        @pl.when(me == DY - 1)
        def _():
            HY[n, 1] = zface

    load_v.wait()

    def pack(x, c):
        for s in range(SPECIES):
            tile = V[0, s, x + 1]
            FY[0, 0, x, s:s + 1, :] = tile[0:1, :]
            FY[0, 1, x, s:s + 1, :] = tile[NY - 1:NY, :]
        return c

    lax.fori_loop(0, NX, pack, 0)
    pl.semaphore_wait(barrier, DY - 1 + DX - 1)

    def copy_x(n, up):
        return pltpu.make_async_remote_copy(
            src_ref=V.at[n, :, NX if up else 1],
            dst_ref=V.at[n, :, 0 if up else NX + 1],
            send_sem=sx.at[n, up],
            recv_sem=rx.at[n, up],
            device_id=at_x(gx + 1 if up else gx - 1),
            device_id_type=MESH,
        )

    def copy_y(n, up, c):
        part = pl.ds(c * CX, CX)
        return pltpu.make_async_remote_copy(
            src_ref=FY.at[n, up, part],
            dst_ref=HY.at[n, 1 - up, part],
            send_sem=sy.at[n, up, c],
            recv_sem=ry.at[n, up, c],
            device_id=at_y(me + 1 if up else me - 1),
            device_id_type=MESH,
        )

    def has(axis_up):
        axis, up = axis_up
        if axis == "x":
            return gx < DX - 1 if up else gx > 0
        return me < DY - 1 if up else me > 0

    def send_x(n, up):
        @pl.when(has(("x", up)))
        def _():
            copy_x(n, up).start()

    def send_y(n, c):
        for up in (0, 1):
            @pl.when(has(("y", up)))
            def _():
                copy_y(n, up, c).start()

    def recv_x(n, up):
        @pl.when(has(("x", 1 - up)))
        def _():
            copy_x(n, up).wait_recv()

    def recv_y(n, c):
        for up in (0, 1):
            @pl.when(has(("y", 1 - up)))
            def _():
                copy_y(n, up, c).wait_recv()

    send_x(0, 0)
    send_x(0, 1)
    for c in ORDER:
        send_y(0, c)

    for load in small:
        load.wait()
    eye = (iota((64, 128), 1) == iota((64, 128), 0)).astype(F32)
    NF[me] = dot(north_ref[...], eye)
    EF[gx] = dot(east_ref[...], eye)

    def n1(k):
        return pltpu.make_async_remote_copy(
            NF.at[me], NF.at[me], sn1, rn1,
            device_id=at_y(gy * GA + lax.rem(ga + k, GA)), device_id_type=MESH)

    def n2(k):
        part = pl.ds(gy * GA, GA)
        return pltpu.make_async_remote_copy(
            NF.at[part], NF.at[part], sn2, rn2,
            device_id=at_y(lax.rem(gy + k, GY) * GA + ga), device_id_type=MESH)

    def e1(k):
        return pltpu.make_async_remote_copy(
            EF.at[gx], EF.at[gx], se1, re1,
            device_id=at_x(xh * ZL + lax.rem(zl + k, ZL)), device_id_type=MESH)

    def e2(k):
        part = pl.ds(xh * ZL, ZL)
        return pltpu.make_async_remote_copy(
            EF.at[part], EF.at[part], se2, re2,
            device_id=at_x(lax.rem(xh + k, DX // ZL) * ZL + zl), device_id_type=MESH)

    for k in range(1, GA):
        n1(k).start()
    for k in range(1, ZL):
        e1(k).start()

    def taken(ref, send, recv):
        return pltpu.make_async_remote_copy(
            ref, ref, send, recv, device_id=at_y(lax.rem(me + 1, DY)), device_id_type=MESH)

    load_t.wait()
    load_f.wait()

    def rates(x, c):
        inverse = 1.0 / T[x]
        for k in range(SPECIES):
            K[k, x] = (0.5 * pre_ref[k]) * jnp.exp((-energy_ref[k]) * inverse)
        for d in range(3):
            F[d, x] = 0.25 * F[d, x]
        return c

    lax.fori_loop(0, NX, rates, 0)

    def splat(s, c):
        for k in range(SPECIES):
            PC[s * SPECIES + k] = jnp.full((8, 128), prod_ref[s, k], F32)
        for a in range(RANK_S):
            CC[s * RANK_S + a] = jnp.full((8, 128), comp_ref[a, s], F32)
        return c

    lax.fori_loop(0, SPECIES, splat, 0)

    spot = iota((32, 256), 1)
    pick = (iota((32, 256), 0) == (spot >> 7) * 16 + (spot & 15)).astype(F32)
    VT[...] = dot_tn(vert_ref[...], pick)

    row = iota((NY, NZ), 0)
    lane = iota((NY, NZ), 1)

    def advance(n, x, last):
        vs = [V[n, s, x + 1] for s in range(SPECIES)]
        react = [K[k, x] * vs[k] * vs[(k + 1) % SPECIES] for k in range(SPECIES)]
        fx, fy, fz = F[0, x], F[1, x], F[2, x]
        for s in range(SPECIES):
            v = vs[s]
            xp, xm = V[n, s, x + 2], V[n, s, x]
            up = jnp.broadcast_to(HY[n, 1, x, s:s + 1, :], (NY, NZ))
            down = jnp.broadcast_to(HY[n, 0, x, s:s + 1, :], (NY, NZ))
            yp = jnp.where(row == NY - 1, up, pltpu.roll(v, NY - 1, 0))
            ym = jnp.where(row == 0, down, pltpu.roll(v, 1, 0))
            zp = jnp.where(lane == NZ - 1, 0.0, pltpu.roll(v, NZ - 1, 1))
            zm = jnp.where(lane == 0, 0.0, pltpu.roll(v, 1, 1))
            half = 0.5 * diff_ref[s]
            total = (1.0 - 6.0 * half) * v + half * ((xp + xm) + (yp + ym) + (zp + zm))
            total = total - (fx * (xp - xm) + fy * (yp - ym) + fz * (zp - zm))
            made = PC[s * SPECIES] * react[0]
            for k in range(1, SPECIES):
                made = made + PC[s * SPECIES + k] * react[k]
            total = total + made
            V[n + 1, s, x + 1] = total
            if not last:
                FY[n + 1, 0, x, s:s + 1, :] = total[0:1, :]
                FY[n + 1, 1, x, s:s + 1, :] = total[NY - 1:NY, :]

    def step(n, c, send=True):
        last = n == 3
        recv_y(n, c)
        if c == 0:
            recv_x(n, 1)
        if c == CHUNKS - 1:
            recv_x(n, 0)

        def body(i, carry):
            advance(n, c * CX + i, last)
            return carry

        lax.fori_loop(0, CX, body, 0)
        if not last:
            if c == 0:
                send_x(n + 1, 0)
            if c == CHUNKS - 1:
                send_x(n + 1, 1)
            if send:
                send_y(n + 1, c)
        else:
            save(c).start()

    def save(c):
        return pltpu.make_async_copy(
            V.at[4, :, pl.ds(1 + c * CX, CX)],
            final_ref.at[:, pl.ds(c * CX, CX)],
            out_sem.at[c])

    step(0, ORDER[0])
    taken(NF.at[pl.ds(0, GA - 1)], sn1, rn1).wait()
    for k in range(1, GY):
        n2(k).start()
    taken(EF.at[pl.ds(0, ZL - 1)], se1, re1).wait()
    for k in range(1, DX // ZL):
        e2(k).start()
    for c in ORDER[1:]:
        step(0, c)
    def squash(x, carry):
        vs = [V[2, s, x + 1] for s in range(SPECIES)]
        for a in range(RANK_S):
            total = CC[a] * vs[0]
            for s in range(1, SPECIES):
                total = total + CC[s * RANK_S + a] * vs[s]
            S[a, x] = total
        return carry

    def project(c):
        where = ((iota((CX, NY, 256), 2) & 127) >> 4) == iota((CX, NY, 256), 1)
        part = pl.ds(c * CX, CX)

        def one(a, carry):
            out = dot(S[a, part].reshape(CX * NY, NZ), VT[...]).reshape(CX, NY, 256)
            out = jnp.sum(jnp.where(where, out, 0.0), axis=1)
            for d in range(2):
                PB[a * 2 + d, c * CX:(c + 1) * CX, :] = out[:, d * 128:(d + 1) * 128]
            return carry

        lax.fori_loop(0, RANK_S, one, 0)

    for c in ORDER:
        step(1, c, send=c in EARLY)
        lax.fori_loop(c * CX, (c + 1) * CX, squash, 0)
        project(c)

    def each_y(start):
        for g in (2, 1, 3, 0):
            def go(o, carry, g=g):
                start(lax.rem(gy + o, GY) * GA + lax.rem(ga + g, GA))
                return carry
            lax.fori_loop(0 if g else 1, GY, go, 0)

    def to_y(src, dst, send, recv):
        def start(j):
            pltpu.make_async_remote_copy(
                src.at[j], dst.at[me], send, recv, device_id=at_y(j), device_id_type=MESH).start()
        each_y(start)

    def each_x(start):
        for g in (2, 1, 3, 0):
            def go(o, carry, g=g):
                start(lax.rem(xh + g, DX // ZL) * ZL + lax.rem(zl + o, ZL))
                return carry
            lax.fori_loop(0 if g else 1, ZL, go, 0)

    def to_x(src, dst, send, recv):
        def start(m):
            pltpu.make_async_remote_copy(
                src.at[m], dst.at[gx], send, recv, device_id=at_x(m), device_id_type=MESH).start()
        each_x(start)

    def done_y(ref, send, recv):
        taken(ref.at[pl.ds(0, DY - 1)], send, recv).wait()

    def done_x(ref, send, recv):
        taken(ref.at[pl.ds(0, DX - 1)], send, recv).wait()

    to_x(PB, G, sp, rp)
    G[gx] = PB[gx]
    keep = pltpu.make_async_copy(V.at[2, :, pl.ds(1, NX)], snap_ref, out_sem.at[CHUNKS])
    keep.start()
    for c in LATE:
        send_y(2, c)
    for c in EARLY:
        step(2, c, send=False)

    taken(NF.at[pl.ds(0, GA * (GY - 1))], sn2, rn2).wait()
    taken(EF.at[pl.ds(0, ZL * (DX // ZL - 1))], se2, re2).wait()
    done_x(G, sp, rp)
    east = EF[...].reshape(DX * NX, 128)
    pairs = dot_tn(east, G[...].reshape(DX * NX, 128))
    for j in range(DY):
        QB[j] = pairs[2 * j:2 * j + 2, :]
    to_y(QB, H, sq, rq)
    H[me] = QB[me]
    for c in EARLY:
        send_y(3, c)
    for c in LATE:
        step(2, c, send=False)

    done_y(H, sq, rq)
    own_y = (iota((DY, NY, 128), 2) >> 4) == iota((DY, NY, 128), 1)
    blocks = []
    for b in range(2):
        spread_h = jnp.broadcast_to(H[:, b:b + 1, :], (DY, NY, 128))
        blocks.append(jnp.where(own_y, spread_h, 0.0).reshape(DY * NY, 128))
    north = NF[...].reshape(DY * NY, 128)
    core = dot_tn(north, jnp.concatenate(blocks, axis=1))
    piece = jnp.zeros((128, 128), F32)
    slot = iota((128, 128), 1) >> 4
    c_low = iota((128, 128), 0) & 1
    parts = []
    for b in range(2):
        part = core[:, b * 128:(b + 1) * 128]
        for shift in (64, 32, 16):
            part = part + pltpu.roll(part, shift, 1)
        parts.append(part)
        piece = piece + jnp.where(slot == b * 2 + c_low, part, 0.0)
    out = dot(north, jnp.concatenate(parts, axis=1))
    for b in range(2):
        block = out[:, b * 128:(b + 1) * 128].reshape(DY, NY, 128)
        MB[:, b, :] = jnp.sum(jnp.where(own_y, block, 0.0), axis=1)
    MB[:, 2, :] = jnp.sum(piece[:64].reshape(DY, 2, 128), axis=1)
    MB[:, 3, :] = jnp.zeros((DY, 128), F32)
    to_y(MB, Q8, sm, rm)
    Q8[me] = MB[me]
    for c in LATE:
        send_y(3, c)
    step(3, ORDER[0])

    QS[64:, :] = jnp.zeros((64, 128), F32)
    done_y(Q8, sm, rm)
    for j in range(DY):
        QS[2 * j:2 * j + 2, :] = Q8[j, 0:2, :]
    UB[...] = dot(EF[...].reshape(DX * NX, 128), QS[...]).reshape(DX, NX, 128)
    to_x(UB, W, su, ru)
    W[gx] = UB[gx]
    for j in range(DY):
        CS[j // 2, j % 2] = Q8[j, 2:3, :]
    home = lax.rem(gx, 2) * 8 + gx // 2

    def core_go(m):
        pltpu.make_async_remote_copy(
            CS.at[m], CO.at[home], sc, rc, device_id=at_x(m), device_id_type=MESH).start()

    each_x(core_go)
    CO[home] = CS[gx]

    for c in ORDER[1:]:
        step(3, c)

    done_x(W, su, ru)
    own_row = (iota((NY, 128), 1) >> 4) == iota((NY, 128), 0)

    def rebuild(a, carry):
        left = []
        for d in range(2):
            rows = []
            for x in range(NX):
                copies = jnp.broadcast_to(W[a * 2 + d, x:x + 1, :], (NY, 128))
                rows.append(jnp.where(own_row, copies, 0.0))
            left.append(jnp.concatenate(rows, axis=0))
        rec_ref[a] = dot_nt(jnp.concatenate(left, axis=1), VT[...]).reshape(NX, NY, NZ)
        return carry

    lax.fori_loop(0, RANK_S, rebuild, 0)

    taken(CO.at[pl.ds(0, DX - 1)], sc, rc).wait()
    result = jnp.zeros((8, 256), F32)
    src_lane = iota((128, 256), 0)
    dst_lane = iota((128, 256), 1)
    b_out, c_out, d_out = dst_lane >> 6, (dst_lane >> 5) & 1, dst_lane & 31
    want = ((b_out & 1) * 2 + c_out) * 16 + (d_out & 15)
    for d in range(2):
        for b in range(2):
            here = jnp.logical_and((b_out >> 1) == b, (d_out >> 4) == d)
            choose = jnp.logical_and(src_lane == want, here).astype(F32)
            result = result + dot(CO[d * 8:(d + 1) * 8, b].reshape(8, 128), choose)
    for i in range(8):
        core_ref[i] = result[:, i * 32:(i + 1) * 32]

    for n in range(4):
        for up in (0, 1):
            @pl.when(has(("x", up)))
            def _():
                copy_x(n, up).wait_send()

            @pl.when(has(("y", up)))
            def _():
                for c in range(CHUNKS):
                    copy_y(n, up, c).wait_send()
    for c in range(CHUNKS):
        save(c).wait()
    keep.wait()


def finish(final_ref, snap_ref, rec_ref, comp_ref, final_hbm, resid_hbm, RES, sem):
    out = pltpu.make_async_copy(final_ref, final_hbm, sem.at[CHUNKS])
    out.start()

    def spill(c):
        return pltpu.make_async_copy(
            RES.at[:, pl.ds(c * CX, CX)], resid_hbm.at[:, pl.ds(c * CX, CX)], sem.at[c])

    def subtract(x, carry):
        rs = [rec_ref[a, x] for a in range(RANK_S)]
        for s in range(SPECIES):
            total = snap_ref[s, x]
            for a in range(RANK_S):
                total = total - comp_ref[a, s] * rs[a]
            RES[s, x] = total
        return carry

    for c in range(CHUNKS):
        lax.fori_loop(c * CX, (c + 1) * CX, subtract, 0)
        spill(c).start()
    for c in range(CHUNKS):
        spill(c).wait()
    out.wait()


def body(v, flow, temp, diff, pre, energy, prod, east, north, vert, comp):
    vmem = pl.BlockSpec(memory_space=pltpu.VMEM)
    hbm = pl.BlockSpec(memory_space=pltpu.HBM)
    smem = pl.BlockSpec(memory_space=pltpu.SMEM)
    field = (SPECIES, NX, NY, NZ)
    dma = pltpu.SemaphoreType.DMA
    tiles = lambda n: pltpu.VMEM((n, 8, 128), F32)
    comp_t = comp.T
    v, flow, temp, east, north, vert, diff, pre, energy, prod, comp = [
        pltpu.with_memory_space_constraint(a, pltpu.HBM)
        for a in (v, flow, temp, east, north, vert.T, diff, pre, energy, prod, comp_t)]
    final, snap, rec, core = pl.pallas_call(
        kernel,
        out_shape=(
            jax.ShapeDtypeStruct(field, F32),
            jax.ShapeDtypeStruct(field, F32),
            jax.ShapeDtypeStruct((RANK_S, NX, NY, NZ), F32),
            jax.ShapeDtypeStruct((8, 8, 32), F32),
        ),
        in_specs=[hbm] * 3 + [smem] * 5 + [hbm] * 3,
        out_specs=(vmem,) * 4,
        scratch_shapes=[
            pltpu.VMEM((5, SPECIES, NX + 2, NY, NZ), F32),
            pltpu.VMEM((3, NX, NY, NZ), F32),
            pltpu.VMEM((NX, NY, NZ), F32),
            pltpu.VMEM(field, F32),
            tiles(SPECIES * SPECIES),
            tiles(SPECIES * RANK_S),
            pltpu.VMEM((4, 2, NX, SPECIES, NZ), F32),
            pltpu.VMEM((4, 2, NX, SPECIES, NZ), F32),
            pltpu.VMEM((RANK_S, NX, NY, NZ), F32),
            pltpu.VMEM((NZ, 256), F32),
            tiles(DY),
            pltpu.VMEM((DX, NX, 128), F32),
            pltpu.VMEM((DX, NX, 128), F32),
            pltpu.VMEM((DX, NX, 128), F32),
            pltpu.VMEM((DY, 2, 128), F32),
            pltpu.VMEM((DY, 2, 128), F32),
            pltpu.VMEM((DY, 4, 128), F32),
            pltpu.VMEM((DY, 4, 128), F32),
            pltpu.VMEM((DX, NX, 128), F32),
            pltpu.VMEM((DX, NX, 128), F32),
            pltpu.VMEM((DX, 2, 1, 128), F32),
            pltpu.VMEM((DX, 2, 1, 128), F32),
            pltpu.VMEM((128, 128), F32),
            pltpu.VMEM((NX, 64), F32), pltpu.VMEM((NY, 64), F32), pltpu.VMEM((32, NZ), F32),
            dma((6,)),
            dma((2 * CHUNKS,)),
            dma((4, 2)), dma((4, 2)), dma((4, 2, CHUNKS)), dma((4, 2, CHUNKS)),
        ] + [dma] * 18,
        compiler_params=pltpu.CompilerParams(
            collective_id=0, has_side_effects=True, vmem_limit_bytes=48 << 20),
        name="flow_tucker",
    )(v, flow, temp, diff, pre, energy, prod, comp, east, north, vert)
    final, resid = pl.pallas_call(
        finish,
        out_shape=(jax.ShapeDtypeStruct(field, F32),) * 2,
        in_specs=[vmem] * 3 + [smem],
        out_specs=(hbm, hbm),
        scratch_shapes=[pltpu.VMEM(field, F32), dma((CHUNKS + 1,))],
        compiler_params=pltpu.CompilerParams(vmem_limit_bytes=16 << 20),
        name="finish",
    )(final, snap, rec, comp)
    return final, resid, core.transpose(1, 0, 2).reshape(8, 4, 2, 32)


def solution(mesh):
    rows = ("gy", "ga")
    field = P(None, "gx", rows, None)
    in_specs = (
        field, field, P("gx", rows, None), P(), P(), P(), P(),
        P("gx", None), P(rows, None), P(), P(),
    )
    return jax.shard_map(
        body, mesh=mesh, in_specs=in_specs, out_specs=(field, field, field), check_vma=False)
```
